256 devices in a mesh: comp: 2 (over core), tile: 16 (over y, x), row: 8 (over z).
Axes of the slice: x: 4, y: 4, z: 8, core: 2. Of those that a mesh axis runs over, the one named last changes fastest.
Arguments:
- state: bfloat16 [2, 16, 512, 12288], P('comp', 'tile', 'row'), may hold values from -8 to 8
- pairs: int32 [2, 2048], replicated, may hold values from 0 to 2047, as said below
- wet: int32 [16], P('tile'), may hold values 0 or 1
- mix_weight: bfloat16 [2, 8, 32, 16], replicated, may hold values from -1 to 1
- depth_weight: float32 [3, 7, 7, 192], replicated, may hold values from -0.875 to 0.875
- norm_gain: float32 [3, 192], replicated, may hold values from 0.1 to 1.9
- inner_weight: bfloat16 [3, 192, 768], replicated, may hold values from -0.4375 to 0.4375
- outer_weight: bfloat16 [3, 768, 192], replicated, may hold values from -0.21875 to 0.21875
Outputs:
- next_state: bfloat16 [2, 16, 512, 12288], P('comp', 'tile', 'row')
The draws below stay inside these ranges and needn't reach their ends.
Inputs may be any that keep to these rules, and one draw needn't show every extreme that they name: Each row pairs[s] is a permutation of the 2048 blocks of the other section, and a block's partner lies in the same band of 64 tile rows. Within one band, the 16 blocks of tile q of one section receive exactly 1 block from that band of each tile of the other section.
All inputs are finite; a program needn't handle non-finite values. No bound on the sum of `wet` on one device may be relied on, other than what follows from the above.
Results may differ from the reference program's by a relative error of at most 0.0053.
Values may be sent and summed in bfloat16 or wider, within the bound.
A program may use at most 64 MiB of HBM per device.

```python
import math
import jax
import jax.numpy as jnp
from jax import lax

C = 192
HID = 768
IC = 128
G = 8
TH = 512
TW = 64
BH = 16
BW = 16
TILES_DEV = 1
RH = 64
RBD = 4
NRB = 32
NCB = 4
IG = 16
TILES = 16
NBLK = 2048
N_TILE = 16


def draw_state(key, part):
    key_base, key_chan, key_cell = jax.random.split(key, 3)
    shape_full = (2, TILES, TH, TW, C)
    base = jax.random.normal(key_base, shape_full, jnp.float32)
    channel_scale = jnp.exp(jax.random.uniform(key_chan, (C,), jnp.float32, math.log(0.3), math.log(3.0)))
    cell_scale = jnp.exp(jax.random.uniform(key_cell, (2, TILES, TH, TW, 1), jnp.float32, math.log(0.3), math.log(3.0)))
    values = jnp.clip(base * channel_scale * cell_scale, -8.0, 8.0)
    return values.reshape(2, TILES, TH, TW * C).astype(jnp.bfloat16)


def draw_pairs(key, part):
    per_dev = TILES_DEV * RBD * NCB
    peer = per_dev // N_TILE
    total = per_dev * N_TILE
    bands = TH // RH

    def band_ids(band):
        position = jnp.arange(total, dtype=jnp.int32)
        owner = position // per_dev
        local = position % per_dev
        tile_local = local // (RBD * NCB)
        block_row = local // NCB % RBD
        block_col = local % NCB
        return ((owner * TILES_DEV + tile_local) * NRB + band * RBD + block_row) * NCB + block_col

    def one_band(band_key):
        key_src, key_slot = jax.random.split(band_key)
        src_perm = jax.vmap(lambda single: jax.random.permutation(single, per_dev))(jax.random.split(key_src, N_TILE))
        sources = (jnp.arange(N_TILE, dtype=jnp.int32)[:, None] * per_dev + src_perm.astype(jnp.int32)).reshape(N_TILE, N_TILE, peer)
        incoming = sources.transpose(1, 0, 2).reshape(N_TILE, per_dev)
        slot_perm = jax.vmap(lambda single: jax.random.permutation(single, per_dev))(jax.random.split(key_slot, N_TILE))
        return jnp.take_along_axis(incoming, slot_perm.astype(jnp.int32), 1).reshape(total)

    def one_section(section_key):
        row_out = jnp.zeros((NBLK,), jnp.int32)
        band_keys = jax.random.split(section_key, bands)
        for band in range(bands):
            ids = band_ids(band)
            picked = one_band(band_keys[band])
            row_out = row_out.at[ids].set(jnp.take(ids, picked))
        return row_out
    section_keys = jax.random.split(jax.random.fold_in(key, 17), 2)
    return jnp.stack([one_section(section_keys[0]), one_section(section_keys[1])]).astype(jnp.int32)


def place_ends(result, key, least, largest):
    spot = [jax.random.randint(jax.random.fold_in(key, axis), (), 0, length) for axis, length in enumerate(result.shape)]
    main_axis = result.shape.index(max(result.shape))
    beside = spot[:main_axis] + [(spot[main_axis] + 1) % result.shape[main_axis]] + spot[main_axis + 1:]
    return result.at[tuple(spot)].set(least).at[tuple(beside)].set(largest)


def bell_draw(rng, extent, scale, bound, held_as=jnp.bfloat16):
    values = jax.random.normal(rng, extent, jnp.float32) * scale
    return jnp.minimum(jnp.maximum(values, -bound), bound).astype(held_as)


def setup_inputs(seed: int = 0) -> dict:
    arg_keys = jax.random.split(jax.random.key(seed), 9)
    state = draw_state(jax.random.fold_in(arg_keys[8], 71), 0)
    pairs = draw_pairs(jax.random.fold_in(arg_keys[8], 71), 0)
    wet = place_ends((jax.random.randint(arg_keys[2], (TILES,), 0, 3) < 2).astype(jnp.int32), jax.random.fold_in(arg_keys[2], 1), 0, 1)
    mix_weight = bell_draw(arg_keys[3], (2, G, 2 * IG, IG), (2 * IG) ** -0.5, 1.0)
    depth_weight = bell_draw(arg_keys[4], (3, 7, 7, C), 49 ** -0.5, 0.875, jnp.float32)
    norm_gain = jnp.clip(1.0 + 0.18 * jax.random.normal(arg_keys[5], (3, C), jnp.float32), 0.1, 1.9)
    inner_weight = bell_draw(arg_keys[6], (3, C, HID), C ** -0.5, 0.4375)
    outer_weight = bell_draw(arg_keys[7], (3, HID, C), HID ** -0.5, 0.21875)
    return {"state": state, "pairs": pairs, "wet": wet, "mix_weight": mix_weight, "depth_weight": depth_weight, "norm_gain": norm_gain, "inner_weight": inner_weight, "outer_weight": outer_weight}


def block_view(section_state):
    cells = section_state.reshape(TILES, NRB, BH, NCB, BW, C)[..., :IC]
    return cells.transpose(0, 1, 3, 2, 4, 5).reshape(NBLK, BH, BW, IC)

def spread_norm_tile(field, depth, gain):
    padded = jnp.pad(field, ((3, 3), (3, 3), (0, 0)))
    spread = jnp.zeros((TH, TW, C), jnp.float32)
    for row_off in range(7):
        for col_off in range(7):
            spread = spread + padded[row_off:row_off + TH, col_off:col_off + TW, :].astype(jnp.float32) * depth[row_off, col_off]
    average = lax.optimization_barrier(jnp.mean(spread, -1, keepdims=True))
    centred = spread - average
    variance = lax.optimization_barrier(jnp.mean(centred * centred, -1, keepdims=True))
    normed = (centred * lax.rsqrt(variance + 1e-06) * gain).astype(jnp.bfloat16)
    return normed.reshape(TH * TW, C)

def project_rows(normed, inner, outer):
    hidden = jax.nn.gelu(jnp.dot(normed, inner, preferred_element_type=jnp.float32), approximate=True).astype(jnp.bfloat16)
    return jnp.dot(hidden, outer, preferred_element_type=jnp.float32)

def reference(state, pairs, wet, mix_weight, depth_weight, norm_gain, inner_weight, outer_weight):
    results = []
    for section in range(2):
        other_blocks = block_view(state[1 - section])
        partners = jnp.take(other_blocks, pairs[section], axis=0).reshape(TILES, NRB, NCB, BH, BW, IC)
        partners = partners.transpose(0, 1, 3, 2, 4, 5).reshape(TILES, TH, NCB, BW, IC)
        if section == 0:
            factors = jnp.ones((TILES,), jnp.float32)
            layers = [0, 1]
        else:
            factors = wet.astype(jnp.float32)
            layers = [2]
        mixing = mix_weight[section].astype(jnp.float32)

        def per_tile(inputs, layers=layers, mixing=mixing):
            tile_flat, partner_rows, factor = inputs
            cells = tile_flat.reshape(TH, NCB, BW, C)
            own_int = cells[..., :IC]
            joined = jnp.concatenate([own_int.reshape(TH, NCB, BW, G, IG), partner_rows.reshape(TH, NCB, BW, G, IG)], -1).astype(jnp.float32)
            mixed = jnp.einsum('hcbgi,gio->hcbgo', joined, mixing).reshape(TH, NCB, BW, IC)
            merged = (own_int.astype(jnp.float32) + mixed).astype(jnp.bfloat16)
            field = jnp.concatenate([merged, cells[..., IC:]], -1).reshape(TH, TW, C)
            for layer in layers:
                normed = spread_norm_tile(field, depth_weight[layer], norm_gain[layer])
                update = project_rows(normed, inner_weight[layer], outer_weight[layer])
                field = (field.reshape(TH * TW, C).astype(jnp.float32) + factor * update).astype(jnp.bfloat16).reshape(TH, TW, C)
            return field.reshape(TH, TW * C)
        results.append(lax.map(per_tile, (state[section], partners, factors)))
    return jnp.stack(results)
```

```python
import jax
import jax.numpy as jnp
from jax import lax
from jax.experimental import pallas as pl
from jax.experimental.pallas import tpu as pltpu
from jax.sharding import PartitionSpec as P

F32, BF16 = jnp.float32, jnp.bfloat16
C, NP = 192, 32
R = 8
TILES = 16
MESH = pl.DeviceIdType.MESH

TAPS = ((3, 3), (1, 1), (5, 5), (4, 2), (2, 0), (6, 4), (0, 6))
CUBE = (0.7978845608028654 * 0.044715) ** (1 / 3)
LINEAR = 0.7978845608028654 / CUBE


def iota(shape, dim):
    return lax.broadcasted_iota(jnp.int32, shape, dim)


def mask(cond):
    return cond.astype(F32).astype(BF16)


def dot(a, b):
    return jnp.dot(a, b, preferred_element_type=F32)


def cat(a, b):
    return jnp.concatenate([a, b], 1)


def turn(v):
    return pltpu.roll(v, 64, 1)


def parts(v):
    a = v.astype(BF16)
    r = v - a.astype(F32)
    b = r.astype(BF16)
    return a, b, (r - b.astype(F32)).astype(BF16)


def prep(dw, gain, inner, outer_t, t_ref, w1_ref, w2_ref):
    r, c = iota((C, 512), 0), iota((C, 512), 1)
    low, high = r < 128, r >= 128
    ea = mask((low & (c == r)) | (high & ((c == r + 128) | (c == r + 256))))
    eb = mask((low & (c == r + 128)) | (high & ((c == r + 192) | (c == r + 320))))
    for a in range(7):
        w = dw[a].astype(BF16)
        wa, wb = dot(w, ea), dot(w, eb)
        for j, (ba, bb) in enumerate(TAPS):
            row = wa[ba:ba + 1] + wb[bb:bb + 1]
            for n in range(2):
                t_ref[n * 49 + a * 7 + j] = jnp.broadcast_to(row[:, 256 * n:256 * n + 256], (8, 256)).astype(BF16)
    r, c = iota((C, C), 0), iota((C, C), 1)
    diag = jnp.where(r == c, jnp.broadcast_to(gain[...], (C, C)), 0.0)
    w = inner[...]
    scaled = sum(dot(p, w) for p in parts(diag)) * (CUBE * C ** 0.5)
    scaled = scaled.astype(BF16)
    none = jnp.zeros((64, 768), BF16)
    w1_ref[0, 0:192] = scaled
    w1_ref[0, 192:256] = none
    w1_ref[1, 0:128] = scaled[:128]
    w1_ref[1, 128:192] = none
    w1_ref[1, 192:256] = scaled[128:]
    r, c = iota((C, 256), 0), iota((C, 256), 1)
    o = outer_t[...]
    for n, e in enumerate((c == r, ((r < 128) & (c == r)) | ((r >= 128) & (c == r + 64)))):
        w2_ref[n] = lax.dot_general(o, mask(e), (((0,), (0,)), ((), ())), preferred_element_type=F32).astype(BF16)


def consts(shift_ref, half_ref, d_ref, j_ref):
    m, c = iota((NP, 160), 0), iota((NP, 160), 1)
    step = jnp.where(c < 32, 0, jnp.where(c < 64, -1, jnp.where(c < 96, 1, jnp.where(c < 128, -2, 2))))
    shift_ref[...] = mask(c % 32 == m + step)
    c = iota((8, 256), 1)
    half_ref[0] = mask(c % 128 < 64)
    half_ref[1] = mask(c % 128 >= 64)
    r, c = iota((256, 256), 0), iota((256, 256), 1)
    for n in range(2):
        inside = (lambda i: i < 192) if n == 0 else (lambda i: (i < 128) | (i >= 192))
        both = inside(r) & inside(c)
        d_ref[n] = jnp.where(both, jnp.where(r == c, 191.0 / 64, -1.0 / 64), 0.0).astype(BF16)
        j_ref[n] = mask(both)


def push(stack, terms):
    n = 1
    while stack and stack[-1][0] == n:
        terms = [u + v for u, v in zip(stack.pop()[1], terms)]
        n *= 2
    stack.append((n, terms))


def total(stack):
    out = stack[-1][1]
    for _, t in stack[-2::-1]:
        out = [u + v for u, v in zip(t, out)]
    return out


def spread(x_ref, s_ref, row, t_ref, n, shift_ref, half_ref):
    groups = []
    for g0 in range(0, 4, 2):
        acc = [[], []]
        for a in range(7):
            w = [t_ref[n * 49 + a * 7 + j] for j in range(7)]
            for g in range(2):
                x = x_ref[row + a, 8 * (g0 + g):8 * (g0 + g) + 8]
                s = s_ref[row + a, 8 * (g0 + g):8 * (g0 + g) + 8]
                push(acc[g], [x * w[d] + s * w[3 + d] for d in range(3)] + [s * w[6]])
        groups += [total(acc[0]), total(acc[1])]
        yield None
    sets = [jnp.concatenate([g[d] for g in groups], 0) for d in range(3)]
    if n == 0:
        two = jnp.concatenate([g[3] for g in groups], 0)
        none = jnp.zeros((NP, 128), BF16)
        sets += [cat(two[:, :128], none), cat(none, two[:, 128:])]
    else:
        for h in range(2):
            sets.append(jnp.concatenate([g[3] * half_ref[h] for g in groups], 0))
    yield dot(shift_ref[...], jnp.concatenate(sets, 0))


def gelu(z):
    z = z.astype(BF16)
    t = jnp.tanh((z * z + jnp.asarray(LINEAR, BF16)) * z)
    return z * t + z


def project(sp0, sp1, sp2, d_ref, j_ref, w1_ref, w2_ref):
    a, b = cat(sp0, sp2), cat(sp1, sp2)
    oa, ob = dot(a, d_ref[0]), dot(b, d_ref[1])
    yield None
    cen = [oa[:, :128], ob[:, :128], oa[:, 128:] + ob[:, 128:]]
    sq = [v.astype(BF16) for v in cen]
    sq = [v * v for v in sq]
    va, vb = dot(cat(sq[0], sq[2]), j_ref[0]), dot(cat(sq[1], sq[2]), j_ref[1])
    yield None
    var = [va[:, :128], vb[:, :128], va[:, 128:] + vb[:, 128:]]
    n = [(c * lax.rsqrt(v + 9e-6 * C)).astype(BF16) for c, v in zip(cen, var)]
    yield None
    out = []
    for i in range(2):
        lhs = cat(n[i], n[2])
        u = None
        for h in range(3):
            hid = gelu(dot(lhs, w1_ref[i, :, 256 * h:256 * h + 256]))
            yield None
            v = dot(hid, w2_ref[i, 256 * h:256 * h + 256])
            u = v if u is None else u + v
        out.append(u)
    yield [out[0][:, :128], out[1][:, :128], out[0][:, 128:] + out[1][:, 128:]]


def weave(*runs):
    live = [[r[0], r[1], 0, r[-1]] for r in runs]
    last = [None] * len(live)
    while True:
        open_ = [i for i, s in enumerate(live) if s[2] < s[1]]
        if not open_:
            return last
        i = min(open_, key=lambda i: (live[i][2] + 1) / live[i][3])
        last[i] = next(live[i][0])
        live[i][2] += 1


def mixing(mix, out_ref):
    r, c = iota((32, 256), 0), iota((32, 256), 1)
    wide = dot(mix.astype(F32).reshape(128, 32).astype(BF16), mask((c % 16 == r % 16) & (c // 128 == r // 16)))
    r, c = iota((128, 256), 0), iota((128, 256), 1)
    wide = jnp.where((c % 128) // 16 == r // 16, wide, 0.0).astype(BF16)
    same = mask(iota((128, 128), 0) == iota((128, 128), 1))
    out_ref[...] = lax.dot_general(wide, same, (((0,), (0,)), ((), ())), preferred_element_type=F32).astype(BF16)


def aligned(i, n):
    return pl.multiple_of(i * n, n)


def kernel(state, pairs, wet, mix_in, depth_in, gain_in, inner_in, outer_in, out01, out2,
           flat, blocks, send, recv, x01, s01, x2, s2, y01, t01, y2, t2, r01, r2, sp2_all, sp_a, sp_b, sp2_a, sp2_b, edge_out, edge_in,
           pair_s, pick_s, wet_s, mix, depth, gain, inner, outer, mixer, taps, w1, w2, shift, half, centre, ones,
           in_sem, state_sem, send_sem, recv_sem, halo_send, halo_recv, edge_send, edge_recv,
           share_send, share_recv, give_send, give_recv):
    section, tile, band = lax.axis_index("comp"), lax.axis_index("tile"), lax.axis_index("row")
    other = 1 - section
    first_layer = 2 * section
    bands = lax.axis_size("row")
    has_up, has_down = band > 0, band < bands - 1
    lo = iota((8, 128), 1) < 64

    def state_load(i):
        rows = pl.ds(aligned(i, 16), 16)
        return pltpu.make_async_copy(state.at[rows], flat.at[rows], state_sem.at[i, 0])

    loads = [pltpu.make_async_copy(s, d, in_sem.at[i]) for i, (s, d) in enumerate((
        (pairs, pair_s), (mix_in, mix), (wet, wet_s), (gain_in, gain),
        (depth_in.at[first_layer], depth.at[0]), (depth_in.at[1], depth.at[1]),
        (inner_in.at[first_layer], inner.at[0]), (inner_in.at[1], inner.at[1]),
        (outer_in.at[first_layer], outer.at[0]), (outer_in.at[1], outer.at[1])))]
    loads[0].start()
    for i in range(4):
        state_load(i).start()

    barrier = pltpu.get_barrier_semaphore()

    @pl.loop(0, TILES)
    def _(q):
        pl.semaphore_signal(barrier, inc=1, device_id={"comp": other, "tile": q}, device_id_type=MESH)

    @pl.when(has_up)
    def _():
        pl.semaphore_signal(barrier, inc=1, device_id={"row": band - 1}, device_id_type=MESH)

    @pl.when(has_down)
    def _():
        pl.semaphore_signal(barrier, inc=1, device_id={"row": band + 1}, device_id_type=MESH)

    for copy in loads[1:]:
        copy.start()

    loads[0].wait()

    @pl.loop(0, TILES)
    def _(q):
        pick = jnp.int32(0)
        for j in range(16):
            v = pair_s[other, q * 128 + band * 16 + j]
            pick = pick + jnp.where(lax.shift_right_logical(v, 7) == tile, v & 15, 0)
        pick_s[q] = pick

    @pl.loop(0, 4)
    def _(br):
        state_load(br).wait()

        @pl.loop(0, 4)
        def _(bc):
            for p in range(8):
                v = []
                for k in range(3):
                    lane = pl.multiple_of((bc * 8 + p) * 384 + 128 * k, 128)
                    v.append(flat[pl.ds(aligned(br, 16), 16), pl.ds(lane, 128)].astype(F32))
                for h in range(2):
                    n0, n1, n2 = (u[8 * h:8 * h + 8] for u in v)
                    for k, u in enumerate((n0, turn(jnp.where(lo, n2, n1)), jnp.where(lo, n1, n2))):
                        blocks[br * 4 + bc, k, pl.ds(64 * h + p, 8, stride=8)] = u

    def exchange(q, slot):
        return pltpu.make_async_remote_copy(
            src_ref=send.at[q], dst_ref=recv.at[slot], send_sem=send_sem.at[q], recv_sem=recv_sem.at[slot],
            device_id={"comp": other, "tile": q}, device_id_type=MESH)

    pl.semaphore_wait(barrier, TILES + jnp.where(has_up, 1, 0) + jnp.where(has_down, 1, 0))

    @pl.loop(0, TILES + 1)
    def _(i):
        @pl.when(i < TILES)
        def _():
            q = (tile + 1 + i) % TILES
            pick = pick_s[q]
            send[q] = cat(blocks[pick, 0], blocks[pick, 1]).astype(BF16)

        @pl.when(i > 0)
        def _():
            exchange((tile + i) % TILES, tile).start()

    def put2(x, s, r, v):
        for ref, u in ((x, v), (s, turn(v))):
            u = u.astype(BF16)
            ref[r + 1, :, 0:128] = u
            ref[r, :, 128:256] = u

    @pl.loop(0, 64)
    def _(r):
        v = jnp.concatenate([blocks[(r // 16) * 4 + bc, 2, pl.ds(aligned(r % 16, 8), 8)] for bc in range(4)], 0)
        put2(x2, s2, r + 3, v)
        for side, first in ((0, 0), (1, 61)):
            @pl.when((r >= first) & (r < first + 3))
            def _():
                edge_out[0, side, r - first] = v.astype(BF16)

    def edge(n):
        up = pltpu.make_async_remote_copy(
            src_ref=edge_out.at[n, 0], dst_ref=edge_in.at[n, 1], send_sem=edge_send.at[n, 0], recv_sem=edge_recv.at[n, 1],
            device_id={"row": band - 1}, device_id_type=MESH)
        down = pltpu.make_async_remote_copy(
            src_ref=edge_out.at[n, 1], dst_ref=edge_in.at[n, 0], send_sem=edge_send.at[n, 1], recv_sem=edge_recv.at[n, 0],
            device_id={"row": band + 1}, device_id_type=MESH)
        return up, down

    def halo(x, n):
        up = pltpu.make_async_remote_copy(
            src_ref=x.at[3:6], dst_ref=x.at[67:70], send_sem=halo_send.at[n, 0], recv_sem=halo_recv.at[n, 1],
            device_id={"row": band - 1}, device_id_type=MESH)
        down = pltpu.make_async_remote_copy(
            src_ref=x.at[64:67], dst_ref=x.at[0:3], send_sem=halo_send.at[n, 1], recv_sem=halo_recv.at[n, 0],
            device_id={"row": band + 1}, device_id_type=MESH)
        return up, down

    def start(pair):
        pl.when(has_up)(pair[0].start)
        pl.when(has_down)(pair[1].start)

    def finish(pair):
        up, down = pair

        @pl.when(has_up)
        def _():
            up.wait_send()
            down.wait_recv()

        @pl.when(has_down)
        def _():
            down.wait_send()
            up.wait_recv()

    def edge_rows(x, s, n):
        for side in range(2):
            for q in range(3):
                put2(x, s, 67 * side + q, edge_in[n, side, q].astype(F32))

    def halo_rows(x, s):
        for r in (0, 1, 2, 67, 68, 69):
            v = x[r]
            s[r] = cat(v[:, 128:], v[:, :128])

    zero = jnp.zeros((NP, 256), BF16)
    for side, inside in ((0, has_up), (1, has_down)):
        @pl.when(jnp.logical_not(inside))
        def _():
            for q in range(3):
                x01[67 * side + q] = zero
                y01[0, 67 * side + q] = zero
                for n in range(2):
                    edge_in[n, side, q] = zero[:, :128]
    start(edge(0))

    for copy in loads[1:]:
        copy.wait()
    mixing(mix[section], mixer)
    consts(shift, half, centre, ones)

    @pl.loop(0, 2)
    def _(n):
        prep(depth.at[n], gain.at[pl.ds(jnp.where(n == 0, first_layer, 1), 1)], inner.at[n], outer.at[n],
             taps.at[n], w1.at[n], w2.at[n])

    def conv2_rows(i):
        for q in range(0, 4, 2):
            for v in spread(x2, s2, 4 * i + q + 1, taps.at[0], 1, shift, half):
                pass
            v = v.astype(BF16)
            sp2_all[4 * i + q], sp2_all[4 * i + q + 1] = v[:, :128], v[:, 128:]

    @pl.loop(1, 15)
    def _(i):
        conv2_rows(i)
    finish(edge(0))
    edge_rows(x2, s2, 0)

    @pl.loop(0, 2)
    def _(i):
        conv2_rows(15 * i)

    @pl.loop(0, TILES)
    def _(u):
        exchange(u, u).wait_recv()

    def couple(br):
        own, lhs = [], []
        for i in range(4):
            b = br * 4 + i
            got = recv[lax.shift_right_logical(pair_s[section, tile * 128 + band * 16 + b], 7)]
            for k in range(2):
                c = blocks[b, k]
                own.append(c)
                lhs.append(cat(c.astype(BF16), got[:, 128 * k:128 * k + 128]))
        mixed = dot(jnp.concatenate(lhs, 0), mixer[...])
        for i in range(4):
            c0, c1 = (own[2 * i + k] + mixed[128 * (2 * i + k):128 * (2 * i + k) + 128] for k in range(2))
            at = pl.ds(8 * i, 8)
            for ref, u in ((x01, cat(c0, c1).astype(BF16)), (s01, cat(c1, c0).astype(BF16))):
                for q in range(16):
                    ref[3 + br * 16 + q, at] = u[8 * q:8 * q + 8]

    @pl.loop(0, 2)
    def _(i):
        couple(3 * i)
    start(halo(x01, 0))

    @pl.loop(1, 3)
    def _(i):
        couple(i)

    bufs = (sp_a, sp2_a), (sp_b, sp2_b)

    def block(n, x, s, xx, ss, factor, store):
        def conv(r0, sp, sp2):
            for q in range(0, R, 2):
                for i in range(2):
                    for v in spread(x, s, r0 + q + i, taps.at[n], 0, shift, half):
                        if v is None:
                            yield None
                    sp[q + i] = v.astype(BF16)
                    yield None
                if n:
                    for v in spread(xx, ss, r0 + q + 1, taps.at[n], 1, shift, half):
                        if v is None:
                            yield None
                    v = v.astype(BF16)
                    sp2[q], sp2[q + 1] = v[:, :128], v[:, 128:]
                    yield None

        def products(r0, sp, sp2):
            a = sp[...].reshape(R * NP, 256)
            c2 = (sp2[...] if n else sp2_all[pl.ds(r0, R)]).reshape(R * NP, 128)
            for v in project(a[:, :128], a[:, 128:], c2, centre, ones, w1.at[n], w2.at[n]):
                yield None
            for q in range(R):
                f = x[r0 + 3 + q].astype(F32)
                f = [f[:, :128], f[:, 128:], xx[r0 + 4 + q, :, 0:128].astype(F32)]
                store(r0 + q, [u + factor * w[NP * q:NP * q + NP] for u, w in zip(f, v)])
                yield None

        return conv, products, (9 if n else 6) * (R // 2), 10 + R

    def to_next(row, c):
        r = row + 3
        y01[0, r], t01[0, r] = cat(c[0], c[1]).astype(BF16), cat(c[1], c[0]).astype(BF16)
        put2(y2.at[0], t2.at[0], r, c[2])

    def to_result(row, c):
        r01[row], r2[row] = cat(c[0], c[1]).astype(BF16), c[2].astype(BF16)

    def arrive_first():
        finish(halo(x01, 0))
        halo_rows(x01, s01)

    def arrive_second():
        @pl.when(section == 0)
        def _():
            finish(halo(y01.at[0], 1))
            halo_rows(y01.at[0], t01.at[0])
            finish(edge(1))
            edge_rows(y2.at[0], t2.at[0], 1)

        @pl.when(section == 1)
        def _():
            share_arrive(2)

    def share(piece):
        low, high = ((16, 27), (27, 43), (43, 54))[piece]
        return [pltpu.make_async_remote_copy(
            src_ref=ref.at[0, first:high], dst_ref=ref.at[1, first:high],
            send_sem=share_send.at[piece, k], recv_sem=share_recv.at[piece, k],
            device_id={"comp": 1}, device_id_type=MESH)
            for k, (ref, first) in enumerate(((y01, low), (t01, low), (y2, max(low, 17)), (t2, max(low, 17))))]

    def first_order(i):
        return jnp.where(i < 5, i + 1, jnp.where(i == 5, 0, jnp.where(i == 6, 7, 6))) * R

    def share_start(piece):
        for copy in share(piece):
            copy.start()

    def share_arrive(piece):
        for copy in share(piece):
            copy.wait_recv()

    def second_order(i):
        edges = jnp.where(i == 0, 1, jnp.where(i == 1, 6, jnp.where(i == 2, 0, 7)))
        return jnp.where(section == 0, edges, i + 2) * R

    def keep(i):
        rows = pl.ds(pl.multiple_of(second_order(i), R), R)
        return [pltpu.make_async_copy(r.at[rows], o.at[rows], state_sem.at[i, k]) for k, (r, o) in enumerate(((r01, out01), (r2, out2)))]

    def give(i):
        rows = pl.ds(aligned(i + 2, R), R)
        return [pltpu.make_async_remote_copy(
            src_ref=r.at[rows], dst_ref=o.at[rows], send_sem=give_send.at[i, k], recv_sem=give_recv.at[i, k],
            device_id={"comp": 0}, device_id_type=MESH) for k, (r, o) in enumerate(((r01, out01), (r2, out2)))]

    def second_done(i):
        @pl.when(section == 0)
        def _():
            for copy in keep(i):
                copy.start()

        @pl.when(section == 1)
        def _():
            for copy in give(i):
                copy.start()

    own = [pltpu.make_async_copy(y01.at[0, 3:67], out01, in_sem.at[0]),
           pltpu.make_async_copy(y2.at[0, 4:68, :, 0:128], out2, in_sem.at[1])]
    scale = 0.5 / CUBE
    factor = jnp.where(section == 0, 1.0, wet_s[0].astype(F32)) * scale
    conv_1, products_1, conv_steps_1, steps = block(0, x01, s01, x2, s2, factor, to_next)
    conv_2, products_2, conv_steps_2, _ = block(
        1, y01.at[section], t01.at[section], y2.at[section], t2.at[section], scale, to_result)

    def first(i, side):
        weave((conv_1(first_order(i + 1), *bufs[1 - side]), conv_steps_1), (products_1(first_order(i), *bufs[side]), steps))

    def second(i, side):
        weave((conv_2(second_order(i + 1), *bufs[1 - side]), conv_steps_2), (products_2(second_order(i), *bufs[side]), steps))
        second_done(i)

    weave((conv_1(first_order(0), *bufs[0]), conv_steps_1))

    @pl.loop(0, 3)
    def _(i):
        pl.when(i == 2)(arrive_first)
        first(2 * i, 0)
        first(2 * i + 1, 1)
        for piece in range(2):
            @pl.when((section == 0) & (i == piece))
            def _():
                share_start(piece)
    first(6, 0)

    @pl.when(section == 0)
    def _():
        for side in range(2):
            for q in range(3):
                edge_out[1, side, q] = y2[0, 4 + 61 * side + q, :, 0:128]
        start(halo(y01.at[0], 1))
        start(edge(1))

    @pl.when(section == 1)
    def _():
        share_arrive(0)
        share_arrive(1)
    weave((conv_2(second_order(0), *bufs[0]), conv_steps_2, 2 * conv_steps_2), (products_1(first_order(7), *bufs[1]), steps))

    @pl.when(section == 0)
    def _():
        share_start(2)

    @pl.when(section == 1)
    def _():
        for copy in own:
            copy.start()

    @pl.loop(0, 1)
    def _(i):
        second(2 * i, 0)
        arrive_second()
        second(2 * i + 1, 1)
    second(2, 0)
    weave((products_2(second_order(3), *bufs[1]), steps))
    second_done(3)

    @pl.when(section == 0)
    def _():
        for piece in range(3):
            for copy in share(piece):
                copy.wait_send()
        for i in range(4):
            for copy in keep(i):
                copy.wait()
            for copy in give(i):
                copy.wait_recv()

    @pl.when(section == 1)
    def _():
        for copy in own:
            copy.wait()
        for i in range(4):
            for copy in give(i):
                copy.wait_send()

    @pl.loop(0, TILES)
    def _(q):
        exchange(q, q).wait_send()


def to_columns(a_ref, b_ref, out, flat, tmp, sem):
    lo = iota((8, 128), 1) < 64
    count = out.shape[0] // 16

    def store(i):
        rows = pl.ds(aligned(i, 16), 16)
        return pltpu.make_async_copy(flat.at[rows], out.at[rows], sem.at[i])

    @pl.loop(0, count)
    def _(i):
        @pl.loop(0, 16, unroll=4)
        def _(r):
            a, c2 = a_ref[i * 16 + r].astype(F32), b_ref[i * 16 + r].astype(F32)
            for bc in range(4):
                for k, c in enumerate((a[:, :128], a[:, 128:], c2)):
                    tmp[bc, k, pl.ds(aligned(r, 8), 8)] = c[8 * bc:8 * bc + 8]

        for bc in range(4):
            for p in range(8):
                n = [[], [], []]
                for h in range(2):
                    c0, c1, c2 = (tmp[bc, k, pl.ds(64 * h + p, 8, stride=8)] for k in range(3))
                    c1 = turn(c1)
                    for k, u in enumerate((c0, jnp.where(lo, c2, c1), jnp.where(lo, c1, c2))):
                        n[k].append(u)
                for k in range(3):
                    lane = (bc * 8 + p) * 384 + 128 * k
                    flat[pl.ds(aligned(i, 16), 16), lane:lane + 128] = jnp.concatenate(n[k], 0).astype(BF16)
        store(i).start()

    @pl.loop(0, count)
    def _(i):
        store(i).wait()


def on_device(state, pairs, wet, mix, depth, gain, inner, outer):
    rows, lanes = state.shape[-2:]
    anywhere = pl.BlockSpec(memory_space=pl.ANY)
    vm, dma = pltpu.VMEM, pltpu.SemaphoreType.DMA
    wide, double = vm((70, NP, 256), BF16), vm((72, NP, 256), BF16)
    result = pl.pallas_call(
        kernel,
        out_shape=[jax.ShapeDtypeStruct((rows, NP, 256), BF16), jax.ShapeDtypeStruct((rows, NP, 128), BF16)],
        in_specs=[pl.BlockSpec(memory_space=pltpu.HBM)] * 8,
        out_specs=[anywhere] * 2,
        scratch_shapes=[
            vm((rows, lanes), BF16), vm((16, 3, 128, 128), F32), vm((TILES, 128, 256), BF16), vm((TILES, 128, 256), BF16),
            wide, wide, double, double, vm((2, 70, NP, 256), BF16), vm((2, 70, NP, 256), BF16),
            vm((2, 72, NP, 256), BF16), vm((2, 72, NP, 256), BF16), vm((rows, NP, 256), BF16), vm((rows, NP, 128), BF16),
            vm((rows, NP, 128), BF16),
            vm((R, NP, 256), BF16), vm((R, NP, 256), BF16), vm((R, NP, 128), BF16), vm((R, NP, 128), BF16),
            vm((2, 2, 3, NP, 128), BF16), vm((2, 2, 3, NP, 128), BF16),
            pltpu.SMEM((2, 2048), jnp.int32), pltpu.SMEM((TILES,), jnp.int32), pltpu.SMEM((1,), jnp.int32),
            vm((2, 8, 16, 32), BF16), vm((2, 7, 7, C), F32), vm((3, C), F32), vm((2, C, 768), BF16), vm((2, C, 768), BF16),
            vm((256, 128), BF16), vm((2, 98, 8, 256), BF16), vm((2, 2, 256, 768), BF16), vm((2, 2, 768, 256), BF16),
            vm((NP, 160), BF16), vm((2, 8, 256), BF16), vm((2, 256, 256), BF16), vm((2, 256, 256), BF16),
            dma((10,)), dma((4, 2)), dma((TILES,)), dma((TILES,)), dma((2, 2)), dma((2, 2)), dma((2, 2)), dma((2, 2)),
            dma((3, 4)), dma((3, 4)), dma((4, 2)), dma((4, 2)),
        ],
        compiler_params=pltpu.CompilerParams(collective_id=0, has_side_effects=True, vmem_limit_bytes=36 << 20),
        name="coupled_step",
    )(*(v if v is wet else pltpu.with_memory_space_constraint(v, pltpu.HBM) for v in (
        state.reshape(rows, lanes), pairs, wet, mix.transpose(0, 1, 3, 2), depth, gain, inner, outer.transpose(0, 2, 1))))
    result = pl.pallas_call(
        to_columns,
        out_shape=jax.ShapeDtypeStruct((rows, lanes), BF16),
        in_specs=[pl.BlockSpec(memory_space=pltpu.VMEM)] * 2,
        out_specs=anywhere,
        scratch_shapes=[vm((rows, lanes), BF16), vm((4, 3, 128, 128), F32), dma((rows // 16,))],
        compiler_params=pltpu.CompilerParams(vmem_limit_bytes=16 << 20),
        name="to_columns",
    )(*result)
    return result.reshape(state.shape)


def solution(mesh):
    return jax.shard_map(
        on_device,
        mesh=mesh,
        in_specs=(P("comp", "tile", "row", None), P(), P("tile"), P(), P(), P(), P(), P()),
        out_specs=P("comp", "tile", "row", None),
        check_vma=False,
    )
```
